32 devices in a mesh: ctx: 8 (over y, x, core), fsdp: 4 (over z).
Axes of the slice: x: 2, y: 2, z: 4, core: 2. Of those that a mesh axis runs over, the one named last changes fastest.
Arguments:
- tokens: bfloat16 [4, 1024, 1024], P('fsdp', 'ctx'), may hold values from -6 to 6
- first_gain: bfloat16 [1024], P('fsdp'), may hold values from 0.5 to 1.5
- query_weight: bfloat16 [1024, 1024], P('fsdp'), may hold values from -0.1875 to 0.1875
- key_weight: bfloat16 [1024, 512], P('fsdp'), may hold values from -0.1875 to 0.1875
- value_weight: bfloat16 [1024, 512], P('fsdp'), may hold values from -0.1875 to 0.1875
- output_weight: bfloat16 [1024, 1024], P('fsdp'), may hold values from -4 to 4
- second_gain: bfloat16 [1024], P('fsdp'), may hold values from 0.5 to 1.5
- router_weight: bfloat16 [1024, 16], P('fsdp'), may hold values from -0.25 to 0.25
- expert_in: bfloat16 [1024, 16, 1024], P('fsdp', 'ctx'), may hold values from -0.1875 to 0.1875
- expert_out: bfloat16 [1024, 16, 512], P('fsdp', 'ctx'), may hold values from -1.796875 to 1.796875
- chosen: int32 [4, 1024, 8], P('fsdp', 'ctx'), may hold values from 0 to 15, all different within a row; in each aligned block of 128 rows (0 to 127, 128 to 255, ..., all dimensions but the last counted through in order) at most 64 rows name the same one
- out_grad: bfloat16 [4, 1024, 1024], P('fsdp', 'ctx'), may hold values from -6 to 6
Outputs:
- layer_out: bfloat16 [4, 1024, 1024], P('fsdp', 'ctx')
- tokens_grad: float32 [4, 1024, 1024], P('fsdp', 'ctx')
- first_gain_grad: float32 [1024], P('fsdp')
- query_grad: float32 [1024, 1024], P('fsdp')
- key_grad: float32 [1024, 512], P('fsdp')
- value_grad: float32 [1024, 512], P('fsdp')
- output_weight_grad: float32 [1024, 1024], P('fsdp')
- second_gain_grad: float32 [1024], P('fsdp')
- router_grad: float32 [1024, 16], P('fsdp')
- expert_in_grad: float32 [1024, 16, 1024], P('fsdp', 'ctx')
- expert_out_grad: float32 [1024, 16, 512], P('fsdp', 'ctx')
The draws below stay inside these ranges and needn't reach their ends.
Inputs may be any that keep to these rules, and one draw needn't show every extreme that they name: `chosen`: each token names 8 different experts. In each aligned block of 128 positions of a sequence (the positions on one device) no expert is named by more than 64 tokens, a bound that some block reaches.
All inputs are finite; a program needn't handle non-finite values.
Results may differ from the reference program's by a relative error of at most 0.025.
Values may be sent and summed in bfloat16 or wider, within the bound.
No kernel may reach another device: no remote copies, remote signals or barrier semaphores. Data moves between devices by JAX's collectives and lax.ppermute only.
A program may use at most 192 MiB of HBM per device.

```python
import math
import jax
import jax.numpy as jnp
import numpy as np
from jax import lax

D = 1024
HEADS = 16
KV_HEADS = 8
HEAD_DIM = 64
FF = 512
TOPK = 8
CTX_TOK = 128
EXPERTS = 16
MOST = 64
LEN = 1024
SEQS = 4


def shard_levels(stream_key, dims, pieces, smallest, largest):
    def one(axis_at, blocks):
        draws = jax.random.uniform(jax.random.fold_in(jax.random.fold_in(stream_key, 6), axis_at), (blocks,), jnp.float32, smallest / len(pieces), largest / len(pieces))
        return jnp.repeat(jnp.exp(draws), dims[axis_at] // blocks).reshape((-1,) + (1,) * (len(dims) - axis_at - 1))

    level = one(*pieces[0])
    for cut in pieces[1:]:
        level = level * one(*cut)
    return level


def assign_block(own_key, own, number, rows, number_of, top, most, skew):
    ranking = jax.random.permutation(own_key, number_of)
    crowded, common = shares(number_of, rows * top, most, skew, True), shares(number_of, rows * top, most, skew, False)
    places = jnp.arange(number_of)

    def named(tallies, rotation):
        used = int((tallies > 0).sum())
        fixed = max(1, used // 4)
        shifted = fixed + (places - fixed + rotation * (used - fixed)) % max(1, number_of - fixed)
        return jnp.zeros((number_of,), jnp.int32).at[ranking[jnp.where(places < fixed, places, shifted)]].set(jnp.asarray(tallies, jnp.int32))

    tallies = jnp.where(number % 4 == 0, named(crowded, number // 4), named(common, number - number // 4 - 1))
    mixed = jax.random.permutation(jax.random.fold_in(own, 3), number_of)
    donor, taker = mixed[0:number_of // 2 * 2:2], mixed[1:number_of // 2 * 2:2]
    margin = jnp.minimum(tallies[donor] - 1, most - tallies[taker]) // 2
    margin = jnp.where((donor == ranking[0]) | (taker == ranking[0]) | (tallies[taker] == 0), 0, jnp.maximum(margin, 0))
    shifted = jax.random.randint(jax.random.fold_in(own, 4), (number_of // 2,), 0, 1 << 20) % (margin + 1)
    tallies = tallies.at[donor].add(-shifted).at[taker].add(shifted)
    members = jnp.searchsorted(jnp.cumsum(tallies), jnp.arange(rows * top), side="right").astype(jnp.int32)
    listing = members.reshape(top, rows).T
    listing = listing[jax.random.permutation(jax.random.fold_in(own, 1), rows)]
    rotation = jax.random.randint(jax.random.fold_in(own, 2), (rows, 1), 0, top)
    return jnp.take_along_axis(listing, (jnp.arange(top)[None, :] + rotation) % top, axis=1)


def shares(number_of, total, most, skew, full):
    loads = [(1 << 20) // math.isqrt(rank ** skew) + 1 for rank in range(1, number_of + 1)]
    largest = most if full else min(most, max(-(-total // number_of), total * loads[0] // sum(loads)))
    least = 1 if total - largest >= number_of - 1 else 0
    counts, spare = [largest] + [least] * (number_of - 1), total - largest - least * (number_of - 1)
    while spare > 0:
        candidates = [i for i in range(1, number_of) if counts[i] < largest] or [i for i in range(1, number_of) if counts[i] < most]
        whole, left = sum([loads[i] for i in candidates]), spare
        for i in candidates:
            addition = min(most - counts[i], max(1, left * loads[i] // whole), spare)
            counts[i] = counts[i] + addition
            spare = spare - addition
    return np.array(counts)


def noise(stream_key, extent, width, bound, shards=(), kind=jnp.bfloat16):
    level = shard_levels(stream_key, extent, shards, -0.22, 0.18) if shards else 1.0
    values = jax.random.normal(stream_key, extent, jnp.float32) * width * level
    return jnp.minimum(jnp.maximum(values, -bound), bound).astype(kind)


def setup_inputs(seed: int = 0) -> dict:
    streams_of = jax.random.split(jax.random.key(seed), 13)
    tokens = noise(streams_of[0], (SEQS, LEN, D), 1.0, 6.0, ((0, 4), (1, 8)))
    first_gain = jnp.clip(1.0 + 0.1 * jax.random.normal(streams_of[1], (D,), jnp.float32), 0.5, 1.5).astype(jnp.bfloat16)
    query_weight = noise(streams_of[2], (D, HEADS * HEAD_DIM), D ** -0.5, 0.1875, ((0, 4),))
    key_weight = noise(streams_of[3], (D, KV_HEADS * HEAD_DIM), D ** -0.5, 0.1875, ((0, 4),))
    value_weight = noise(streams_of[4], (D, KV_HEADS * HEAD_DIM), D ** -0.5, 0.1875, ((0, 4),))
    output_weight = noise(streams_of[5], (HEADS * HEAD_DIM, D), 2 ** -0.5, 4.0, ((0, 4),))
    second_gain = jnp.clip(1.0 + 0.1 * jax.random.normal(streams_of[6], (D,), jnp.float32), 0.5, 1.5).astype(jnp.bfloat16)
    router_weight = noise(streams_of[7], (D, EXPERTS), (D // 2) ** -0.5, 0.25, ((0, 4),))
    expert_in = noise(streams_of[8], (D, EXPERTS, 2 * FF), D ** -0.5, 0.1875, ((0, 4), (1, 8)))
    expert_out = noise(streams_of[9], (D, EXPERTS, FF), 0.3, 1.796875, ((0, 4), (1, 8)))
    chosen_keys = jax.random.split(jax.random.fold_in(streams_of[10], 1), SEQS * LEN // CTX_TOK)
    chosen_turns = jax.random.permutation(jax.random.fold_in(streams_of[10], 3), SEQS * LEN // CTX_TOK)
    chosen = jax.vmap(lambda own, number: assign_block(jax.random.fold_in(streams_of[10], 2), own, number, CTX_TOK, EXPERTS, TOPK, MOST, 1))(chosen_keys, chosen_turns).reshape((SEQS, LEN, TOPK))
    out_grad = noise(streams_of[11], (SEQS, LEN, D), 1.0, 6.0, ((0, 4), (1, 8)))
    return dict(tokens=tokens, first_gain=first_gain, query_weight=query_weight, key_weight=key_weight, value_weight=value_weight, output_weight=output_weight, second_gain=second_gain, router_weight=router_weight, expert_in=expert_in, expert_out=expert_out, chosen=chosen, out_grad=out_grad)


EPSILON = 1e-06
RESIDUAL = 0.22
ROPE_BASE = 10000.0
HIGHEST = lax.Precision.HIGHEST

@jax.custom_vjp
def low(v):
    return lax.optimization_barrier(v.astype(jnp.bfloat16)).astype(jnp.float32)

@jax.custom_vjp
def reduced_backward(v):
    return v

def low_keep(v):
    return (low(v), None)

def low_pass(kept, grad):
    return (grad,)

def back_keep(v):
    return (v, None)

def back_low(kept, grad):
    return (low(grad),)
low.defvjp(low_keep, low_pass)
reduced_backward.defvjp(back_keep, back_low)

def product(form, left_arr, right_arr):
    return jnp.einsum(form, left_arr, right_arr, precision=HIGHEST)

def rms_gain(values, gain_vec):
    return values * lax.rsqrt(lax.optimization_barrier(jnp.mean(values * values, axis=-1, keepdims=True)) + EPSILON) * gain_vec

def rotate(values, positions):
    middle = values.shape[-1] // 2
    inverse = ROPE_BASE ** (-jnp.arange(middle, dtype=jnp.float32) / middle)
    angles = positions.astype(jnp.float32)[:, None] * inverse[None, :]
    cosine = jnp.cos(angles)[:, None, :]
    sine_table = jnp.sin(angles)[:, None, :]
    front_half = values[..., :middle]
    back_half = values[..., middle:]
    return jnp.concatenate([front_half * cosine - back_half * sine_table, back_half * cosine + front_half * sine_table], axis=-1)

def attend_sequence(queries, keys, values):
    length = queries.shape[0]
    query_len = min(512, length)
    grouped = queries.reshape(length // query_len, query_len, KV_HEADS, HEADS // KV_HEADS, HEAD_DIM)
    key_pos = jnp.arange(length, dtype=jnp.int32)

    def one_block(operands):
        query_block, first_row = operands
        scores = reduced_backward(product('qgrd,kgd->grqk', query_block, keys) * 0.125)
        query_pos = first_row + jnp.arange(query_len, dtype=jnp.int32)
        scores = jnp.where(key_pos[None, :] <= query_pos[:, None], scores, -1e+30)
        weights = low(jax.nn.softmax(scores, axis=-1))
        return product('grqk,kgd->qgrd', weights, values)
    starts = (jnp.arange(length // query_len, dtype=jnp.int32) * query_len).astype(jnp.int32)
    outputs = lax.map(jax.checkpoint(one_block), (grouped, starts))
    return outputs.reshape(length, HEADS * HEAD_DIM)

def slot_table(seq_chosen):
    length = seq_chosen.shape[0]
    blocks = length // CTX_TOK
    picked = lax.optimization_barrier(jnp.sum((seq_chosen[:, :, None] == jnp.arange(EXPERTS, dtype=jnp.int32)[None, None, :]).astype(jnp.int32), axis=1)).astype(jnp.int32)
    within = picked.reshape(blocks, CTX_TOK, EXPERTS)
    slot_rank = (jnp.cumsum(within, axis=1) - within).astype(jnp.int32).reshape(length, EXPERTS)
    block_of = (jnp.arange(length, dtype=jnp.int32) // CTX_TOK).astype(jnp.int32)
    slot_index = (block_of[:, None] * MOST + slot_rank).astype(jnp.int32)
    capacity = blocks * MOST
    token_ids = jnp.broadcast_to(jnp.arange(length, dtype=jnp.int32)[:, None], (length, EXPERTS))
    expert_ids = jnp.broadcast_to(jnp.arange(EXPERTS, dtype=jnp.int32)[None, :], (length, EXPERTS))
    target = jnp.where(picked > 0, slot_index, capacity).astype(jnp.int32)
    slot_tokens = jnp.zeros((EXPERTS, capacity), jnp.int32).at[expert_ids, target].set(token_ids, mode='drop')
    filled = jnp.zeros((EXPERTS, capacity), jnp.int32).at[expert_ids, target].set(jnp.ones_like(token_ids), mode='drop')
    return (slot_tokens, filled, picked)

def layer(inputs, gain_one, w_query, w_key, w_value, w_output, gain_two, w_router, w_gate_up, w_down, slot_tokens, filled, picked):
    length = inputs.shape[0]
    positions = jnp.arange(length, dtype=jnp.int32)
    normed_one = low(rms_gain(inputs, gain_one))
    query_proj = reduced_backward(product('ld,de->le', normed_one, w_query))
    key_proj = reduced_backward(product('ld,de->le', normed_one, w_key))
    value_proj = reduced_backward(product('ld,de->le', normed_one, w_value))
    queries = low(rotate(query_proj.reshape(length, HEADS, HEAD_DIM), positions))
    keys = low(rotate(key_proj.reshape(length, KV_HEADS, HEAD_DIM), positions))
    values = low(value_proj).reshape(length, KV_HEADS, HEAD_DIM)
    attended = low(reduced_backward(attend_sequence(queries, keys, values)))
    branch = reduced_backward(product('le,ed->ld', attended, w_output))
    hidden = inputs + RESIDUAL * branch
    second_normalized = low(rms_gain(hidden, gain_two))
    logits = reduced_backward(product('ld,de->le', second_normalized, w_router))
    gate_probs = jax.nn.softmax(jnp.where(picked > 0, logits, -1e+30), axis=-1) * picked.astype(jnp.float32)

    def expert(mixture, expert_parts):
        one_in, one_down, slot_row_table, slot_valid, gate_vector = expert_parts
        slot_validity = slot_valid.astype(jnp.float32)
        incoming_rows = reduced_backward(second_normalized[slot_row_table] * slot_validity[:, None])
        gate_up = reduced_backward(product('cd,df->cf', incoming_rows, one_in))
        active = low(jax.nn.silu(gate_up[:, :FF]) * gate_up[:, FF:])
        result = low(reduced_backward(product('cf,df->cd', active, one_down)))
        weight_matrix = gate_vector[slot_row_table] * slot_validity
        return (mixture.at[slot_row_table].add(weight_matrix[:, None] * result), None)
    start_mix = jnp.zeros((length, inputs.shape[1]), jnp.float32)
    mixture, unused = lax.scan(jax.checkpoint(expert), start_mix, (jnp.moveaxis(w_gate_up, 1, 0), jnp.moveaxis(w_down, 1, 0), slot_tokens, filled, gate_probs.T))
    return hidden + RESIDUAL * mixture

def reference(tokens, first_gain, query_weight, key_weight, value_weight, output_weight, second_gain, router_weight, expert_in, expert_out, chosen, out_grad):
    weights = (first_gain.astype(jnp.float32), query_weight.astype(jnp.float32), key_weight.astype(jnp.float32), value_weight.astype(jnp.float32), output_weight.astype(jnp.float32), second_gain.astype(jnp.float32), router_weight.astype(jnp.float32), expert_in.astype(jnp.float32), expert_out.astype(jnp.float32))

    def one_sequence(totals, operands):
        seq_tokens, seq_chosen, seq_grad = operands
        slot_tokens, filled, picked = slot_table(seq_chosen)

        def apply_layer(seq_in, *params):
            return layer(seq_in, *params, slot_tokens, filled, picked)
        result, pullback = jax.vjp(apply_layer, seq_tokens.astype(jnp.float32), *weights)
        gradients = pullback(seq_grad.astype(jnp.float32))
        totals = jax.tree.map(jnp.add, totals, tuple(gradients[1:]))
        return (totals, (result.astype(jnp.bfloat16), gradients[0]))
    zero_grads = tuple((jnp.zeros_like(matrix) for matrix in weights))
    totals, (outputs, input_grads) = lax.scan(one_sequence, zero_grads, (tokens, chosen, out_grad))
    grad_one, grad_query, grad_key, grad_value, grad_output, grad_two, grad_router, grad_in, grad_down = totals
    return (outputs, input_grads, grad_one, grad_query, grad_key, grad_value, grad_output, grad_two, grad_router, grad_in, grad_down)
```

```python
import jax
import jax.numpy as jnp
from jax import lax
from jax.experimental import pallas as pl
from jax.experimental.pallas import tpu as pltpu
from jax.sharding import PartitionSpec as P

HEADS = 16
KV_HEADS = 8
HEAD_DIM = 64
FF = 512
MOST = 64

EPSILON = 1e-06
RESIDUAL = 0.22
ROPE_BASE = 10000.0
BF = jnp.bfloat16
F32 = jnp.float32


def dot(a, b, dims=((1,), (0,))):
    return lax.dot_general(a, b, (dims, ((), ())), preferred_element_type=F32)


def bits_of(size):
    found, bit = [], 1
    while bit < size:
        found.append(bit)
        bit *= 2
    return [1] + found[:0:-1]


def order_of(size):
    places = [0]
    for bit in reversed(bits_of(size)):
        places = places + [place ^ bit for place in places]
    return places


def swap_ctx(value, bit, size):
    return lax.ppermute(value, "ctx", [(i, i ^ bit) for i in range(size)])


def paths_of(size):
    bits = bits_of(size)
    far = bits[1:]
    return bits, (far, far[1:] + far[:1])


def cut_of(width):
    return max(128, (width // 256) * 128)


def gather_half(value, path, bits, size):
    held = []
    for bit in list(path) + [1]:
        other = swap_ctx(value, bit, size)
        axis = sum(1 for seen in held if bits.index(seen) < bits.index(bit))
        value = jnp.stack([value, other], axis=axis)
        held.append(bit)
    return value.reshape((size,) + value.shape[len(bits):])


def gather_ctx(value, size):
    bits, paths = paths_of(size)
    cut = cut_of(value.shape[-1])
    parts = [value[..., :cut], value[..., cut:]]
    return jnp.concatenate(
        [gather_half(part, path, bits, size) for part, path in zip(parts, paths)], axis=-1
    )


def add_low(mine, other):
    return (mine.astype(F32) + other.astype(F32)).astype(BF)


def scatter_ctx(blocks, size):
    bits, paths = paths_of(size)
    half = size // 2
    blocks = add_low(blocks[:half], swap_ctx(blocks[half:], 1, size))
    cut = cut_of(blocks.shape[-1])
    done = []
    for part, path in zip((blocks[..., :cut], blocks[..., cut:]), paths):
        part = part.reshape((2,) * (len(bits) - 1) + part.shape[1:])
        left = bits[1:]
        for bit in reversed(path):
            axis = left.index(bit)
            keep = lax.index_in_dim(part, 0, axis, keepdims=False)
            send = lax.index_in_dim(part, 1, axis, keepdims=False)
            other = swap_ctx(send, bit, size)
            left = [b for b in left if b != bit]
            if left:
                part = add_low(keep, other)
            else:
                part = keep.astype(F32) + other.astype(F32)
        done.append(part)
    return jnp.concatenate(done, axis=-1)


def exchange_ctx(blocks, size):
    return [blocks[0]] + [swap_ctx(blocks[k], k, size) for k in range(1, size)]


def shift_fsdp(value, step, size):
    return lax.ppermute(value, "fsdp", [(i, (i + step) % size) for i in range(size)])


def gather_fsdp(value, size):
    if size != 4:
        return jnp.concatenate(
            [value] + [shift_fsdp(value, k, size) for k in range(1, size)], axis=0
        )
    rows = value.shape[0] // 2
    left = shift_fsdp(value, 1, size)
    right = shift_fsdp(value, -1, size)
    top = shift_fsdp(left[:rows], 1, size)
    low = shift_fsdp(right[rows:], -1, size)
    return jnp.concatenate([value, left, top, low, right], axis=0)


def scatter_fsdp(value, size):
    rows = value.shape[0] // size
    part = [value[k * rows : (k + 1) * rows] for k in range(size)]
    if size != 4:
        total = part[0]
        for k in range(1, size):
            total = total + shift_fsdp(part[k].astype(BF), -k, size).astype(F32)
        return total
    half = rows // 2
    far = part[2].astype(BF)
    top = shift_fsdp(far[:half], 1, size).astype(F32)
    low = shift_fsdp(far[half:], -1, size).astype(F32)
    zero = jnp.zeros_like(top)
    up = (part[3] + jnp.concatenate([top, zero], axis=0)).astype(BF)
    down = (part[1] + jnp.concatenate([zero, low], axis=0)).astype(BF)
    return (
        part[0]
        + shift_fsdp(up, 1, size).astype(F32)
        + shift_fsdp(down, -1, size).astype(F32)
    )


def pick(blocks, index):
    return lax.dynamic_index_in_dim(blocks, index, 0, keepdims=False)


def columns(value, start, width):
    return lax.dynamic_slice_in_dim(value, start, width, value.ndim - 1)


def forward_kernel(q_ref, k_ref, v_ref, qpos_ref, kpos_ref, low_ref, high_ref, lse_ref):
    allowed = kpos_ref[...] <= qpos_ref[...]
    keys = k_ref[...]
    values = v_ref[...]
    for head in range(q_ref.shape[1] // HEAD_DIM):
        cols = slice(head * HEAD_DIM, (head + 1) * HEAD_DIM)
        scores = dot(q_ref[:, cols], keys, ((1,), (1,))) * 0.125
        scores = jnp.where(allowed, scores, -1e30)
        top = jnp.max(scores, axis=-1, keepdims=True)
        weights = jnp.exp(scores - top)
        total = jnp.sum(weights, axis=-1, keepdims=True)
        out = dot(weights.astype(BF), values) / total
        high_ref[:, cols] = out
        low_ref[:, cols] = out.astype(BF)
        lse_ref[:, head : head + 1] = top + jnp.log(total)


def attend(queries, keys, values, qpos, kpos):
    length, wide = queries.shape
    rows = min(256, length)
    heads = wide // HEAD_DIM
    whole = lambda i: (0, 0)
    block = lambda i: (i, 0)
    return pl.pallas_call(
        forward_kernel,
        grid=(length // rows,),
        in_specs=[
            pl.BlockSpec((rows, wide), block),
            pl.BlockSpec((length, HEAD_DIM), whole),
            pl.BlockSpec((length, HEAD_DIM), whole),
            pl.BlockSpec((rows, 1), block),
            pl.BlockSpec((1, length), whole),
        ],
        out_specs=[
            pl.BlockSpec((rows, wide), block),
            pl.BlockSpec((rows, wide), block),
            pl.BlockSpec((rows, heads), block),
        ],
        out_shape=[
            jax.ShapeDtypeStruct((length, wide), BF),
            jax.ShapeDtypeStruct((length, wide), F32),
            jax.ShapeDtypeStruct((length, heads), F32),
        ],
        name="attend",
    )(queries, keys, values, qpos, kpos)


def turn_back(grad, cos, sin):
    middle = HEAD_DIM // 2
    swapped = jnp.concatenate([grad[:, middle:], -grad[:, :middle]], axis=-1)
    return grad * cos + swapped * sin


def backward_kernel(
    q_ref, k_ref, v_ref, qpos_ref, kpos_ref, out_ref, lse_ref, do_ref, qcos_ref, qsin_ref,
    kcos_ref, ksin_ref, dq_ref, dkv_ref, dk_acc, dv_acc,
):
    step = pl.program_id(0)

    @pl.when(step == 0)
    def _():
        dk_acc[...] = jnp.zeros_like(dk_acc)
        dv_acc[...] = jnp.zeros_like(dv_acc)

    allowed = kpos_ref[...] <= qpos_ref[...]
    keys = k_ref[...]
    values = v_ref[...]
    for head in range(q_ref.shape[1] // HEAD_DIM):
        cols = slice(head * HEAD_DIM, (head + 1) * HEAD_DIM)
        query = q_ref[:, cols]
        grad = do_ref[:, cols]
        delta = jnp.sum(grad.astype(F32) * out_ref[:, cols], axis=-1, keepdims=True)
        scores = dot(query, keys, ((1,), (1,))) * 0.125
        probs = jnp.where(allowed, jnp.exp(scores - lse_ref[:, head : head + 1]), 0.0)
        prob_grad = dot(grad, values, ((1,), (1,)))
        score_grad = (probs * (prob_grad - delta)).astype(BF)
        dq = dot(score_grad, keys) * 0.125
        dq_ref[:, cols] = turn_back(dq, qcos_ref[...], qsin_ref[...]).astype(BF)
        dk_acc[...] += dot(score_grad, query, ((0,), (0,)))
        dv_acc[...] += dot(probs.astype(BF), grad, ((0,), (0,)))

    @pl.when(step == pl.num_programs(0) - 1)
    def _():
        dk = turn_back(dk_acc[...] * 0.125, kcos_ref[...], ksin_ref[...])
        dkv_ref[:, :HEAD_DIM] = dk.astype(BF)
        dkv_ref[:, HEAD_DIM:] = dv_acc[...].astype(BF)


def attend_back(queries, keys, values, qpos, kpos, out, lse, grad, cos, sin):
    length, wide = queries.shape
    rows = min(256, length)
    heads = wide // HEAD_DIM
    whole = lambda i: (0, 0)
    block = lambda i: (i, 0)
    return pl.pallas_call(
        backward_kernel,
        grid=(length // rows,),
        in_specs=[
            pl.BlockSpec((rows, wide), block),
            pl.BlockSpec((length, HEAD_DIM), whole),
            pl.BlockSpec((length, HEAD_DIM), whole),
            pl.BlockSpec((rows, 1), block),
            pl.BlockSpec((1, length), whole),
            pl.BlockSpec((rows, wide), block),
            pl.BlockSpec((rows, heads), block),
            pl.BlockSpec((rows, wide), block),
            pl.BlockSpec((rows, HEAD_DIM), block),
            pl.BlockSpec((rows, HEAD_DIM), block),
            pl.BlockSpec((length, HEAD_DIM), whole),
            pl.BlockSpec((length, HEAD_DIM), whole),
        ],
        out_specs=[
            pl.BlockSpec((rows, wide), block),
            pl.BlockSpec((length, 2 * HEAD_DIM), whole),
        ],
        out_shape=[
            jax.ShapeDtypeStruct((length, wide), BF),
            jax.ShapeDtypeStruct((length, 2 * HEAD_DIM), BF),
        ],
        scratch_shapes=[
            pltpu.VMEM((length, HEAD_DIM), F32),
            pltpu.VMEM((length, HEAD_DIM), F32),
        ],
        name="attend_back",
    )(queries, keys, values, qpos, kpos, out, lse, grad, cos, sin, cos, sin)


def turned_columns(weight):
    rows, wide = weight.shape
    halves = weight.reshape(rows, wide // HEAD_DIM, 2, HEAD_DIM // 2)
    return jnp.stack([-halves[:, :, 1], halves[:, :, 0]], axis=2).reshape(rows, wide)


def per_device(
    tokens,
    first_gain,
    query_weight,
    key_weight,
    value_weight,
    output_weight,
    second_gain,
    router_weight,
    expert_in,
    expert_out,
    chosen,
    out_grad,
):
    seqs, rows, width = tokens.shape
    ctx = lax.axis_size("ctx")
    fsdp = lax.axis_size("fsdp")
    c = lax.axis_index("ctx")
    s = lax.axis_index("fsdp")
    experts = router_weight.shape[1]
    local = expert_in.shape[1]
    length = ctx * rows
    slab = width // fsdp
    q_wide = HEADS * HEAD_DIM // ctx
    kv_shared = max(1, ctx // KV_HEADS)
    order = order_of(ctx)
    places = jnp.array(order, jnp.int32)

    def flip(value):
        return jnp.concatenate(
            [columns(value, ((s - j) % fsdp) * slab, slab) for j in range(fsdp)], axis=-1
        )

    def to_places(blocks):
        return jnp.stack([pick(blocks, c ^ place) for place in order], axis=0)

    own = flip(tokens[0])
    own_grad = flip(out_grad[0])
    named = jnp.sum(
        (chosen[0][..., None] == jnp.arange(experts, dtype=jnp.int32)).astype(F32), axis=1
    )
    flags = jnp.pad(named.astype(BF), ((0, 0), (0, 128 - experts)))
    shared_in = gather_ctx(jnp.concatenate([own, flags], axis=-1), ctx).reshape(length, -1)
    all_grad = gather_ctx(own_grad, ctx)
    all_x = shared_in[:, :width].astype(F32)
    all_named = shared_in[:, width : width + experts].astype(F32)

    kv_at = (c // kv_shared) * HEAD_DIM
    packed = jnp.concatenate(
        [
            columns(query_weight, c * q_wide, q_wide),
            columns(key_weight, kv_at, HEAD_DIM),
            columns(value_weight, kv_at, HEAD_DIM),
            router_weight,
            first_gain[:, None],
            second_gain[:, None],
            jnp.zeros((slab, 128 - experts - 2), BF),
        ],
        axis=-1,
    )
    packed = gather_fsdp(packed, fsdp)
    qkv_wide = q_wide + 2 * HEAD_DIM
    w_qkv = packed[:, :qkv_wide]
    w_router = packed[:, qkv_wide : qkv_wide + experts]
    gains = packed[:, qkv_wide + experts : qkv_wide + experts + 2].astype(F32).T
    gain_one = gains[:1]
    gain_two = gains[1:2]
    output_weight, expert_in, expert_out, packed = lax.optimization_barrier(
        (output_weight, expert_in, expert_out, packed)
    )
    w_output = gather_fsdp(output_weight, fsdp)
    w_in = gather_fsdp(expert_in.reshape(slab, -1), fsdp)
    w_out = gather_fsdp(expert_out.reshape(slab, -1), fsdp)

    block_index = c ^ places
    positions = (
        block_index[:, None] * rows + jnp.arange(rows, dtype=jnp.int32)[None, :]
    ).reshape(length)
    inverse = ROPE_BASE ** (-jnp.arange(HEAD_DIM // 2, dtype=F32) / (HEAD_DIM // 2))
    angles = positions.astype(F32)[:, None] * inverse[None, :]
    cos = jnp.tile(jnp.cos(angles), (1, 2))
    sin = jnp.tile(jnp.sin(angles), (1, 2))
    qpos = positions[:, None]
    kpos = positions[None, :]

    r_one = lax.rsqrt(jnp.mean(all_x * all_x, axis=-1, keepdims=True) + EPSILON)
    n_one = (all_x * r_one * gain_one).astype(BF)
    w_turned = turned_columns(w_qkv[:, : q_wide + HEAD_DIM])
    proj = dot(n_one, jnp.concatenate([w_qkv, w_turned], axis=-1))
    q_heads = q_wide // HEAD_DIM
    queries = (
        proj[:, :q_wide] * jnp.tile(cos, (1, q_heads))
        + proj[:, qkv_wide : qkv_wide + q_wide] * jnp.tile(sin, (1, q_heads))
    ).astype(BF)
    keys = (
        proj[:, q_wide : q_wide + HEAD_DIM] * cos + proj[:, qkv_wide + q_wide :] * sin
    ).astype(BF)
    values = proj[:, q_wide + HEAD_DIM : qkv_wide].astype(BF)
    heads_low, heads_high, lse = attend(queries, keys, values, qpos, kpos)

    sent = heads_low.reshape(ctx, rows, q_wide)
    at = [order.index(k) for k in range(ctx)]
    pieces = jnp.stack(exchange_ctx([sent[at[k]] for k in range(ctx)], ctx), axis=0)
    attended = flip(jnp.concatenate([pick(pieces, c ^ m) for m in range(ctx)], axis=-1))
    own_x = own.astype(F32)
    hidden = own_x + RESIDUAL * flip(dot(attended, w_output))
    r_two = lax.rsqrt(jnp.mean(hidden * hidden, axis=-1, keepdims=True) + EPSILON)
    n_two = (hidden * r_two * gain_two).astype(BF)
    all_two = gather_ctx(n_two, ctx)

    def gates(values_low, mask):
        logits = dot(values_low, w_router)
        return jax.nn.softmax(jnp.where(mask > 0, logits, -1e30), axis=-1) * mask

    all_gates = gates(all_two.reshape(length, width), all_named)
    loc_named = columns(all_named, c * local, local).reshape(ctx, rows, local)
    loc_gates = columns(all_gates, c * local, local).reshape(ctx, rows, local)
    before = (
        jnp.arange(rows, dtype=jnp.int32)[:, None] > jnp.arange(rows, dtype=jnp.int32)[None, :]
    ).astype(BF)
    rank = jnp.einsum(
        "tu,jue->jet", before, loc_named.astype(BF), preferred_element_type=F32
    )
    named_t = jnp.swapaxes(loc_named, 1, 2)
    gates_t = jnp.swapaxes(loc_gates, 1, 2)
    slots = jnp.arange(MOST, dtype=F32)[:, None]
    hit = (rank[:, :, None, :] == slots) & (named_t[:, :, None, :] > 0)
    chooser = hit.astype(BF)
    gate_rows = jnp.sum(jnp.where(hit, gates_t[:, :, None, :], 0.0), axis=-1)
    flat = (ctx * MOST, width)
    chunks_x = []
    chunks_gy = []
    for e in range(local):
        chunks_x.append(
            jnp.einsum("jqt,jtd->jqd", chooser[:, e], all_two, preferred_element_type=F32)
            .astype(BF)
            .reshape(flat)
        )
        chunks_gy.append(
            jnp.einsum("jqt,jtd->jqd", chooser[:, e], all_grad, preferred_element_type=F32)
            .reshape(flat)
        )
    moe = 0.0
    back = 0.0
    in_terms = []
    out_terms = []
    gate_terms = []
    for e in range(local):
        x_e = chunks_x[e]
        gy_e = chunks_gy[e]
        w_in_e = w_in[:, e * 2 * FF : (e + 1) * 2 * FF]
        w_out_e = w_out[:, e * FF : (e + 1) * FF]
        g_e = gate_rows[:, e].reshape(ctx * MOST, 1)
        u = dot(x_e, w_in_e)
        gate = u[:, :FF]
        up = u[:, FF:]
        sig = jax.nn.sigmoid(gate)
        swish = gate * sig
        act = (swish * up).astype(BF)
        dy = (RESIDUAL * g_e * gy_e).astype(BF)
        out_terms.append(dot(dy, act, ((0,), (0,))))
        dact = dot(dy, w_out_e)
        dgate = dact * up * (sig * (1.0 + gate * (1.0 - sig)))
        du = jnp.concatenate([dgate, dact * swish], axis=-1).astype(BF)
        in_terms.append(dot(x_e, du, ((0,), (0,))))
        y = dot(act, w_out_e, ((1,), (1,))).astype(BF).astype(F32)
        gate_terms.append(RESIDUAL * jnp.sum(gy_e * y, axis=-1).reshape(ctx, MOST))
        dn = dot(du, w_in_e, ((1,), (1,))).astype(BF).reshape(ctx, MOST, width)
        wy = (g_e * y).astype(BF).reshape(ctx, MOST, width)
        moe = moe + jnp.einsum("jqt,jqd->jtd", chooser[:, e], wy, preferred_element_type=F32)
        back = back + jnp.einsum("jqt,jqd->jtd", chooser[:, e], dn, preferred_element_type=F32)
    dg_slots = jnp.stack(gate_terms, axis=1)
    dg_loc = jnp.sum(jnp.where(hit, dg_slots[..., None], 0.0), axis=2)
    place = (
        jnp.arange(experts, dtype=jnp.int32)[None, :]
        == c * local + jnp.arange(local, dtype=jnp.int32)[:, None]
    ).astype(F32)
    dg_all = jnp.sum(jnp.swapaxes(dg_loc, 1, 2)[..., None] * place, axis=2)
    dg_high = dg_all.astype(BF)
    dg_rest = (dg_all - dg_high.astype(F32)).astype(BF)
    pad = jnp.zeros((ctx, rows, 128 - 2 * experts), BF)
    back = jnp.concatenate([back.astype(BF), dg_high, dg_rest, pad], axis=-1)
    back = scatter_ctx(back, ctx)
    in_grad = scatter_fsdp(jnp.concatenate(in_terms, axis=-1), fsdp).reshape(
        slab, local, 2 * FF
    )
    out_grad_w = scatter_fsdp(jnp.concatenate(out_terms, axis=-1), fsdp).reshape(
        slab, local, FF
    )
    layer_out = flip((hidden + RESIDUAL * scatter_ctx(moe.astype(BF), ctx)).astype(BF))

    dg = back[:, width : width + experts] + back[:, width + experts : width + 2 * experts]
    own_gates = gates(n_two, named)
    dlogits = (
        own_gates * (dg - jnp.sum(own_gates * dg, axis=-1, keepdims=True))
    ).astype(BF)
    dn_two = back[:, :width] + dot(dlogits, w_router, ((1,), (1,)))
    router_term = dot(n_two, dlogits, ((0,), (0,)))
    gain_two_term = jnp.sum(dn_two * hidden * r_two, axis=0)
    pulled = dn_two * gain_two
    dh = (
        own_grad.astype(F32)
        + r_two * pulled
        - hidden * r_two * r_two * r_two * jnp.mean(pulled * hidden, axis=-1, keepdims=True)
    )
    da = flip((RESIDUAL * dh).astype(BF))
    do_own = flip(dot(da, w_output, ((1,), (1,))).astype(BF))
    do_blocks = [columns(do_own, (c ^ k) * q_wide, q_wide) for k in range(ctx)]
    do_pieces = exchange_ctx(do_blocks, ctx)
    do_heads = jnp.concatenate([do_pieces[k] for k in order], axis=0)
    output_term = scatter_fsdp(dot(attended, da, ((0,), (0,))), fsdp)
    output_out = lax.psum(output_term.astype(BF), "ctx").astype(F32)

    dq, dkv = attend_back(
        queries, keys, values, qpos, kpos, heads_high, lse, do_heads, cos, sin
    )
    d_qkv = jnp.concatenate([dq, dkv], axis=-1)
    dn_one = dot(d_qkv, w_qkv, ((1,), (1,))).astype(BF).reshape(ctx, rows, width)
    dn_one = scatter_ctx(dn_one, ctx)
    w_term = dot(n_one, d_qkv, ((0,), (0,)))
    gain_one_term = jnp.sum(w_term * w_qkv.astype(F32), axis=-1, keepdims=True) / gain_one.T
    small = jnp.concatenate(
        [
            w_term,
            router_term,
            gain_one_term,
            gain_two_term[:, None],
            jnp.zeros((width, 128 - experts - 2), F32),
        ],
        axis=-1,
    )
    small = gather_ctx(scatter_fsdp(small, fsdp).astype(BF), ctx)
    where = jnp.array(at, jnp.int32)
    shards = [pick(small, where[c ^ m]).astype(F32) for m in range(ctx)]
    query_out = jnp.concatenate([shard[:, :q_wide] for shard in shards], axis=-1)
    key_parts = [shard[:, q_wide : q_wide + HEAD_DIM] for shard in shards]
    value_parts = [shard[:, q_wide + HEAD_DIM : qkv_wide] for shard in shards]
    key_out = jnp.concatenate(
        [sum(key_parts[i : i + kv_shared]) for i in range(0, ctx, kv_shared)], axis=-1
    )
    value_out = jnp.concatenate(
        [sum(value_parts[i : i + kv_shared]) for i in range(0, ctx, kv_shared)], axis=-1
    )
    rest = jnp.sum(small[:, :, qkv_wide:].astype(F32), axis=0)
    router_out = rest[:, :experts]
    gain_one_out = rest[:, experts]
    gain_two_out = rest[:, experts + 1]

    pulled_one = dn_one * gain_one
    own_r = lax.rsqrt(jnp.mean(own_x * own_x, axis=-1, keepdims=True) + EPSILON)
    tokens_grad = (
        dh
        + own_r * pulled_one
        - own_x * own_r * own_r * own_r
        * jnp.mean(pulled_one * own_x, axis=-1, keepdims=True)
    )
    tokens_grad = flip(tokens_grad)
    return (
        layer_out[None],
        tokens_grad[None],
        gain_one_out,
        query_out,
        key_out,
        value_out,
        output_out,
        gain_two_out,
        router_out,
        in_grad,
        out_grad_w,
    )


def solution(mesh):
    in_specs = (
        P("fsdp", "ctx", None),
        P("fsdp"),
        P("fsdp", None),
        P("fsdp", None),
        P("fsdp", None),
        P("fsdp", None),
        P("fsdp"),
        P("fsdp", None),
        P("fsdp", "ctx", None),
        P("fsdp", "ctx", None),
        P("fsdp", "ctx", None),
        P("fsdp", "ctx", None),
    )
    out_specs = (
        P("fsdp", "ctx", None),
        P("fsdp", "ctx", None),
        P("fsdp"),
        P("fsdp", None),
        P("fsdp", None),
        P("fsdp", None),
        P("fsdp", None),
        P("fsdp"),
        P("fsdp", None),
        P("fsdp", "ctx", None),
        P("fsdp", "ctx", None),
    )
    return jax.shard_map(
        per_device, mesh=mesh, in_specs=in_specs, out_specs=out_specs, check_vma=False
    )
```

```python
import jax
import jax.numpy as jnp
from jax import lax
from jax.experimental import pallas as pl
from jax.experimental.pallas import tpu as pltpu
from jax.sharding import PartitionSpec as P

HEADS = 16
KV_HEADS = 8
HEAD_DIM = 64
FF = 512
MOST = 64

EPSILON = 1e-06
RESIDUAL = 0.22
ROPE_BASE = 10000.0
BF = jnp.bfloat16
F32 = jnp.float32


def dot(a, b, dims=((1,), (0,))):
    return lax.dot_general(a, b, (dims, ((), ())), preferred_element_type=F32)


def order_of(size):
    return list(range(0, size, 2)) + list(range(1, size, 2))


def swap_ctx(value, offset, size):
    return lax.ppermute(value, "ctx", [(i, i ^ offset) for i in range(size)])


def gather_ctx(value, size):
    near = [value] + [swap_ctx(value, k, size) for k in range(2, size, 2)]
    far = [swap_ctx(part, 1, size) for part in near]
    return near + far


def after(value, *others):
    return lax.optimization_barrier((value,) + others)[0]


def scatter_ctx(blocks, size):
    return scatter_far(*scatter_near(blocks, size), size)


def scatter_near(blocks, size):
    half = size // 2
    other = swap_ctx(blocks[half:], 1, size)
    low = [
        (blocks[p].astype(F32) + other[p].astype(F32)).astype(BF) for p in range(1, half)
    ]
    return blocks[0].astype(F32) + other[0].astype(F32), low


def scatter_far(total, low, size):
    for p in range(1, size // 2):
        total = total + swap_ctx(low[p - 1], 2 * p, size).astype(F32)
    return total


def exchange_ctx(blocks, size):
    half = size // 2
    other = swap_ctx(blocks[half:], 1, size)
    pairs = [jnp.stack([blocks[p], other[p]], axis=0) for p in range(half)]
    return jnp.concatenate(
        [pairs[0]] + [swap_ctx(pairs[p], 2 * p, size) for p in range(1, half)], axis=0
    )


def shift_fsdp(value, step, size):
    return lax.ppermute(value, "fsdp", [(i, (i + step) % size) for i in range(size)])


def gather_steps(value, size, here):
    rows = value.shape[0]
    half = rows // 2
    if size == 4:
        came = [shift_fsdp(value, 1, size), shift_fsdp(value, -1, size)]
    else:
        came = [shift_fsdp(value, k, size) for k in range(1, size)]

    def finish(got):
        if size == 4:
            left, right = got
            top = shift_fsdp(left[:half], 1, size)
            low = shift_fsdp(right[half:], -1, size)
            parts = [(value, 0, 0), (left, -1, 0), (right, 1, 0), (top, 2, 0), (low, 2, half)]
        else:
            parts = [(value, 0, 0)] + [(part, -k - 1, 0) for k, part in enumerate(got)]
        whole = jnp.zeros((rows * size,) + value.shape[1:], value.dtype)
        for part, step, extra in parts:
            start = ((here + step) % size) * rows + extra
            whole = lax.dynamic_update_slice_in_dim(whole, part, start, 0)
        return whole

    return came, finish


def scatter_steps(value, size, here):
    rows = value.shape[0] // size
    part = [
        lax.dynamic_slice_in_dim(value, ((here + k) % size) * rows, rows, 0) for k in range(size)
    ]
    if size != 4:
        came = [shift_fsdp(part[k].astype(BF), k, size) for k in range(1, size)]
        return came, lambda got: sum([p.astype(F32) for p in got], part[0].astype(F32))
    half = rows // 2
    far = part[2].astype(BF)
    came = [shift_fsdp(far[:half], 1, size), shift_fsdp(far[half:], -1, size)]

    def finish(got):
        top, low = got
        up = jnp.concatenate(
            [
                (part[1][:half].astype(F32) + top.astype(F32)).astype(BF),
                part[1][half:].astype(BF),
            ],
            axis=0,
        )
        down = jnp.concatenate(
            [
                part[3][:half].astype(BF),
                (part[3][half:].astype(F32) + low.astype(F32)).astype(BF),
            ],
            axis=0,
        )
        return (
            part[0].astype(F32)
            + shift_fsdp(up, 1, size).astype(F32)
            + shift_fsdp(down, -1, size).astype(F32)
        )

    return came, finish


def scatter_fsdp(value, size, here):
    came, finish = scatter_steps(value, size, here)
    return finish(came)


def pick(blocks, index):
    return lax.dynamic_index_in_dim(blocks, index, 0, keepdims=False)


def columns(value, start, width):
    return lax.dynamic_slice_in_dim(value, start, width, value.ndim - 1)


def turn(value, cos, sin):
    middle = HEAD_DIM // 2
    swapped = jnp.concatenate([-value[:, middle:], value[:, :middle]], axis=-1)
    return value * cos + swapped * sin


def forward_kernel(*refs):
    gain_ref, w_ref, cos_ref, sin_ref, qpos_ref, kpos_ref = refs[-13:-7]
    n_ref, q_ref, k_ref, v_ref, low_ref, high_ref, lse_ref = refs[-7:]
    x_refs = refs[:-13]
    length, wide = q_ref.shape
    width = n_ref.shape[1]
    rows = min(256, length)
    small = length // len(x_refs)

    for i, x_ref in enumerate(x_refs):
        at = slice(i * small, (i + 1) * small)
        x = x_ref[:, :width].astype(F32)
        scale = lax.rsqrt(jnp.mean(x * x, axis=-1, keepdims=True) + EPSILON)
        n_one = (x * scale * gain_ref[...]).astype(BF)
        n_ref[at, :] = n_one
        proj = dot(n_one, w_ref[...])
        cos = cos_ref[at, :]
        sin = sin_ref[at, :]
        for head in range(wide // HEAD_DIM):
            cols = slice(head * HEAD_DIM, (head + 1) * HEAD_DIM)
            q_ref[at, cols] = turn(proj[:, cols], cos, sin).astype(BF)
        k_ref[at, :] = turn(proj[:, wide : wide + HEAD_DIM], cos, sin).astype(BF)
        v_ref[at, :] = proj[:, wide + HEAD_DIM :].astype(BF)

    def attend_rows(i, carry):
        at = pl.ds(pl.multiple_of(i * rows, rows), rows)
        allowed = kpos_ref[...] <= qpos_ref[at, :]
        keys = k_ref[...]
        values = v_ref[...]
        for head in range(wide // HEAD_DIM):
            cols = slice(head * HEAD_DIM, (head + 1) * HEAD_DIM)
            scores = dot(q_ref[at, cols], keys, ((1,), (1,))) * 0.125
            scores = jnp.where(allowed, scores, -1e30)
            top = jnp.max(scores, axis=-1, keepdims=True)
            weights = jnp.exp(scores - top)
            total = jnp.sum(weights, axis=-1, keepdims=True)
            out = dot(weights.astype(BF), values) / total
            high_ref[at, cols] = out
            low_ref[at, cols] = out.astype(BF)
            lse_ref[at, head : head + 1] = top + jnp.log(total)
        return carry

    lax.fori_loop(0, length // rows, attend_rows, 0)


def attend(pieces, gain, weight, cos, sin, qpos, kpos, width, wide):
    length = cos.shape[0]
    shapes = [
        ((length, width), BF),
        ((length, wide), BF),
        ((length, HEAD_DIM), BF),
        ((length, HEAD_DIM), BF),
        ((length, wide), BF),
        ((length, wide), F32),
        ((length, wide // HEAD_DIM), F32),
    ]
    return pl.pallas_call(
        forward_kernel,
        out_shape=[jax.ShapeDtypeStruct(shape, kind) for shape, kind in shapes],
        name="attend",
    )(*pieces, gain, weight, cos, sin, qpos, kpos)


def turn_back(grad, cos, sin):
    middle = HEAD_DIM // 2
    swapped = jnp.concatenate([grad[:, middle:], -grad[:, :middle]], axis=-1)
    return grad * cos + swapped * sin


def backward_kernel(*refs):
    (
        q_ref, k_ref, v_ref, qpos_ref, kpos_ref, out_ref, lse_ref, do_ref, cos_ref, sin_ref,
        n_ref, w_ref, gain_ref, extra_ref,
    ) = refs[:14]
    small_ref, dn_ref, d_ref, dk_acc, dv_acc = refs[-5:]
    att_refs = refs[14:-5]
    length, wide = q_ref.shape
    qkv = wide + 2 * HEAD_DIM
    rows = min(256, length)
    small = length // len(att_refs)
    dk_acc[...] = jnp.zeros_like(dk_acc)
    dv_acc[...] = jnp.zeros_like(dv_acc)

    def step(i, carry):
        at = pl.ds(pl.multiple_of(i * rows, rows), rows)
        allowed = kpos_ref[...] <= qpos_ref[at, :]
        keys = k_ref[...]
        values = v_ref[...]
        for head in range(wide // HEAD_DIM):
            cols = slice(head * HEAD_DIM, (head + 1) * HEAD_DIM)
            query = q_ref[at, cols]
            grad = do_ref[at, cols]
            delta = jnp.sum(grad.astype(F32) * out_ref[at, cols], axis=-1, keepdims=True)
            scores = dot(query, keys, ((1,), (1,))) * 0.125
            probs = jnp.where(allowed, jnp.exp(scores - lse_ref[at, head : head + 1]), 0.0)
            prob_grad = dot(grad, values, ((1,), (1,)))
            score_grad = (probs * (prob_grad - delta)).astype(BF)
            dq = dot(score_grad, keys) * 0.125
            d_ref[at, cols] = turn_back(dq, cos_ref[at, :], sin_ref[at, :]).astype(BF)
            dk_acc[...] += dot(score_grad, query, ((0,), (0,)))
            dv_acc[...] += dot(probs.astype(BF), grad, ((0,), (0,)))
        return carry

    lax.fori_loop(0, length // rows, step, 0)
    dk = turn_back(dk_acc[...] * 0.125, cos_ref[...], sin_ref[...])
    d_ref[:, wide : wide + HEAD_DIM] = dk.astype(BF)
    d_ref[:, wide + HEAD_DIM :] = dv_acc[...].astype(BF)
    for j in range(len(att_refs)):
        dn_ref[j] = dot(d_ref[j * small : (j + 1) * small, :], w_ref[...], ((1,), (1,))).astype(BF)
    term = dot(n_ref[...], d_ref[...], ((0,), (0,)))
    small_ref[:, :qkv] = term.astype(BF)
    gain = jnp.sum(term * w_ref[...].astype(F32), axis=-1, keepdims=True) / gain_ref[...]
    total = 0.0
    for j, att_ref in enumerate(att_refs):
        total = total + dot(
            att_ref[...], do_ref[j * small : (j + 1) * small, wide:], ((0,), (0,))
        )
    last = small_ref.shape[1] - 128
    small_ref[:, qkv:last] = total.astype(BF)
    lane = lax.broadcasted_iota(jnp.int32, (term.shape[0], 128), 1)
    small_ref[:, last:] = jnp.where(lane == 127, gain, extra_ref[...]).astype(BF)


def attend_back(queries, keys, values, qpos, kpos, out, lse, grad, cos, sin,
                normed, weight, gain, extra, attended):
    length, wide = queries.shape
    width = normed.shape[1]
    count = len(attended)
    return pl.pallas_call(
        backward_kernel,
        out_shape=[
            jax.ShapeDtypeStruct((width, grad.shape[1] + 2 * HEAD_DIM + 128), BF),
            jax.ShapeDtypeStruct((count, length // count, width), BF),
        ],
        scratch_shapes=[
            pltpu.VMEM((length, wide + 2 * HEAD_DIM), BF),
            pltpu.VMEM((length, HEAD_DIM), F32),
            pltpu.VMEM((length, HEAD_DIM), F32),
        ],
        name="attend_back",
    )(queries, keys, values, qpos, kpos, out, lse, grad, cos, sin, normed, weight, gain,
      extra, *attended)


def front_kernel(*refs):
    at_ref, named_ref, chooser_ref, w_router_ref, w_in_ref = refs[:5]
    x_ref, gy_ref, u_ref, act_ref, dy_ref, gate_ref, term_ref = refs[-7:]
    pieces = refs[5:-7]
    blocks, both, rows = chooser_ref.shape
    local = both // MOST
    slots = blocks * MOST
    for j in range(blocks):
        n_two = pieces[j][...]
        named = named_ref[j * rows : (j + 1) * rows, :]
        logits = jnp.where(named > 0, dot(n_two, w_router_ref[...]), -1e30)
        raised = jnp.exp(logits - jnp.max(logits, axis=-1, keepdims=True))
        gates = raised / jnp.sum(raised, axis=-1, keepdims=True) * named
        high = gates.astype(BF)
        rest = (gates - high.astype(F32)).astype(BF)
        chooser = chooser_ref[j]
        chosen_gates = dot(chooser, high) + dot(chooser, rest)
        x = dot(chooser, n_two).astype(BF)
        gy = dot(chooser, pieces[blocks + j][...])
        lane = lax.broadcasted_iota(jnp.int32, (MOST, chosen_gates.shape[1]), 1)
        for e in range(local):
            at = slice(e * slots + j * MOST, e * slots + (j + 1) * MOST)
            part = slice(e * MOST, (e + 1) * MOST)
            gate = jnp.sum(
                jnp.where(lane == at_ref[0] + e, chosen_gates[part], 0.0),
                axis=-1,
                keepdims=True,
            )
            gate_ref[at, :] = gate
            x_ref[at, :] = x[part]
            gy_ref[at, :] = gy[part].astype(BF)
            dy_ref[at, :] = (RESIDUAL * gate * gy[part]).astype(BF)
    chunk = min(256, slots)
    for e in range(local):
        for i in range(slots // chunk):
            at = slice(e * slots + i * chunk, e * slots + (i + 1) * chunk)
            u = dot(x_ref[at, :], w_in_ref[:, e * 2 * FF : (e + 1) * 2 * FF])
            u_ref[at, :] = u
            gate = u[:, :FF]
            act_ref[at, :] = (gate / (1.0 + jnp.exp(-gate)) * u[:, FF:]).astype(BF)
        at = slice(e * slots, (e + 1) * slots)
        term_ref[:, e * FF : (e + 1) * FF] = dot(
            dy_ref[at, :], act_ref[at, :], ((0,), (0,))
        ).astype(BF)


def expert_front(at, named, chooser, w_router, w_in, pieces):
    blocks, both, rows = chooser.shape
    local = both // MOST
    total = blocks * both
    width = w_in.shape[0]
    smem = pl.BlockSpec(memory_space=pltpu.SMEM)
    vmem = pl.BlockSpec(memory_space=pltpu.VMEM)
    shapes = [
        ((total, width), BF),
        ((total, width), BF),
        ((total, 2 * FF), F32),
        ((total, FF), BF),
        ((total, width), BF),
        ((total, 1), F32),
        ((width, local * FF), BF),
    ]
    return pl.pallas_call(
        front_kernel,
        in_specs=[smem] + [vmem] * (4 + len(pieces)),
        out_specs=[vmem] * 7,
        out_shape=[jax.ShapeDtypeStruct(shape, kind) for shape, kind in shapes],
        name="expert_front",
    )(at, named, chooser, w_router, w_in, *pieces)


def assemble_kernel(*refs):
    at_ref = refs[0]
    query_ref, key_ref, value_ref, output_ref, rest_ref = refs[-5:]
    pieces = refs[1:-5]
    here = at_ref[0]
    even = (here & 1) == 0
    half = len(pieces) // 2
    rest = 0.0
    for p, piece_ref in enumerate(pieces):
        place = here ^ (2 * (p % half) + p // half)
        cols = pl.ds(pl.multiple_of(place * 128, 128), 128)
        query_ref[:, cols] = piece_ref[:, :128].astype(F32)
        output_ref[:, cols] = piece_ref[:, 256:384].astype(F32)
        rest = rest + piece_ref[:, 384:].astype(F32)
    rest_ref[...] = rest
    for p in range(half):
        one = pieces[p][:, 128:256].astype(F32)
        two = pieces[half + p][:, 128:256].astype(F32)
        low = jnp.where(even, one, two)
        high = jnp.where(even, two, one)
        place = (here ^ (2 * p)) // 2
        cols = pl.ds(pl.multiple_of(place * 128, 128), 128)
        key_ref[:, cols] = jnp.concatenate([low[:, :HEAD_DIM], high[:, :HEAD_DIM]], axis=-1)
        value_ref[:, cols] = jnp.concatenate([low[:, HEAD_DIM:], high[:, HEAD_DIM:]], axis=-1)


def assemble(here, pieces):
    rows = pieces[0].shape[0]
    count = len(pieces)
    smem = pl.BlockSpec(memory_space=pltpu.SMEM)
    vmem = pl.BlockSpec(memory_space=pltpu.VMEM)
    widths = [count * 128, count * HEAD_DIM, count * HEAD_DIM, count * 128, 128]
    return pl.pallas_call(
        assemble_kernel,
        in_specs=[smem] + [vmem] * count,
        out_specs=[vmem] * 5,
        out_shape=[jax.ShapeDtypeStruct((rows, wide), F32) for wide in widths],
        name="assemble",
    )(here, *pieces)


def expert_kernel(
    at_ref, u_ref, act_ref, dy_ref, gy_ref, gate_ref, comb_ref, w_in_ref, w_out_ref,
    back_ref, moe_ref, du_ref, dn_ref, wy_ref,
):
    local = w_out_ref.shape[1] // FF
    slots = act_ref.shape[0] // local
    width = dy_ref.shape[1]
    blocks, _, rows = comb_ref.shape
    experts = at_ref[1]
    chunk = min(256, slots)
    lane = lax.broadcasted_iota(jnp.int32, (chunk, 128), 1)
    for e in range(local):
        named = at_ref[0] + e
        for i in range(slots // chunk):
            at = slice(e * slots + i * chunk, e * slots + (i + 1) * chunk)
            w_out = w_out_ref[:, e * FF : (e + 1) * FF]
            y = dot(act_ref[at, :], w_out, ((1,), (1,))).astype(BF).astype(F32)
            wy_ref[at, :] = (gate_ref[at, :] * y).astype(BF)
            dg = RESIDUAL * jnp.sum(gy_ref[at, :].astype(F32) * y, axis=-1, keepdims=True)
            high = dg.astype(BF).astype(F32)
            spread = jnp.where(lane == named, high, 0.0)
            spread = jnp.where(lane == experts + named, dg - high, spread)
            dact = dot(dy_ref[at, :], w_out)
            gate = u_ref[at, :FF]
            up = u_ref[at, FF:]
            sig = 1.0 / (1.0 + jnp.exp(-gate))
            swish = gate * sig
            dgate = dact * up * (sig * (1.0 + gate * (1.0 - sig)))
            du_ref[at, :FF] = dgate.astype(BF)
            du_ref[at, FF:] = (dact * swish).astype(BF)
            w_in = w_in_ref[:, e * 2 * FF : (e + 1) * 2 * FF]
            dn_ref[at, :width] = dot(du_ref[at, :], w_in, ((1,), (1,))).astype(BF)
            dn_ref[at, width:] = spread.astype(BF)
    for j in range(blocks):
        comb = comb_ref[j]
        back = 0.0
        moe = 0.0
        for e in range(local):
            at = slice(e * slots + j * MOST, e * slots + (j + 1) * MOST)
            mine = comb[e * MOST : (e + 1) * MOST, :]
            back = back + dot(mine, dn_ref[at, :], ((0,), (0,)))
            moe = moe + dot(mine, wy_ref[at, :], ((0,), (0,)))
        back_ref[j] = back.astype(BF)
        moe_ref[j] = moe.astype(BF)


def expert_back(at, u, act, dy, gy, gates, comb, w_in, w_out):
    total, width = dy.shape
    blocks, _, rows = comb.shape
    smem = pl.BlockSpec(memory_space=pltpu.SMEM)
    vmem = pl.BlockSpec(memory_space=pltpu.VMEM)
    return pl.pallas_call(
        expert_kernel,
        in_specs=[smem] + [vmem] * 8,
        out_specs=[vmem] * 3,
        out_shape=[
            jax.ShapeDtypeStruct((blocks, rows, width + 128), BF),
            jax.ShapeDtypeStruct((blocks, rows, width), BF),
            jax.ShapeDtypeStruct((total, 2 * FF), BF),
        ],
        scratch_shapes=[
            pltpu.VMEM((total, width + 128), BF),
            pltpu.VMEM((total, width), BF),
        ],
        name="expert_back",
    )(at, u, act, dy, gy, gates, comb, w_in, w_out)


def per_device(
    tokens,
    first_gain,
    query_weight,
    key_weight,
    value_weight,
    output_weight,
    second_gain,
    router_weight,
    expert_in,
    expert_out,
    chosen,
    out_grad,
):
    seqs, rows, width = tokens.shape
    ctx = lax.axis_size("ctx")
    fsdp = lax.axis_size("fsdp")
    c = lax.axis_index("ctx")
    s = lax.axis_index("fsdp")
    experts = router_weight.shape[1]
    local = expert_in.shape[1]
    length = ctx * rows
    slab = width // fsdp
    q_wide = HEADS * HEAD_DIM // ctx
    kv_shared = max(1, ctx // KV_HEADS)
    order = order_of(ctx)
    places = jnp.array(order, jnp.int32)

    def to_places(blocks):
        return jnp.stack([pick(blocks, c ^ place) for place in order], axis=0)

    own = tokens[0]
    own_grad = out_grad[0]
    named = jnp.sum(
        (chosen[0][..., None] == jnp.arange(experts, dtype=jnp.int32)).astype(F32), axis=1
    )
    flags = jnp.pad(named.astype(BF), ((0, 0), (0, 128 - experts)))
    shared_in = gather_ctx(jnp.concatenate([own, flags], axis=-1), ctx)
    all_named = jnp.concatenate(
        [part[:, width : width + experts] for part in shared_in], axis=0
    ).astype(F32)

    kv_at = (c // kv_shared) * HEAD_DIM
    packed = jnp.concatenate(
        [
            columns(query_weight, c * q_wide, q_wide),
            columns(key_weight, kv_at, HEAD_DIM),
            columns(value_weight, kv_at, HEAD_DIM),
            router_weight,
            first_gain[:, None],
            second_gain[:, None],
            jnp.zeros((slab, 128 - experts - 2), BF),
        ],
        axis=-1,
    )
    came_p, finish_p = gather_steps(packed, fsdp, s)
    packed = finish_p(came_p)
    qkv_wide = q_wide + 2 * HEAD_DIM
    w_qkv = packed[:, :qkv_wide]
    w_router = packed[:, qkv_wide : qkv_wide + experts]
    gains = packed[:, qkv_wide + experts : qkv_wide + experts + 2].astype(F32).T
    gain_one = gains[:1]
    gain_two = gains[1:2]
    first_half = c % 2 == 0
    half_out = jnp.where(
        first_half, output_weight[:, : width // 2], output_weight[:, width // 2 :]
    )
    came_o, finish_o = gather_steps(half_out, fsdp, s)
    expert_in, expert_out = lax.optimization_barrier((expert_in, expert_out, *came_p))[:2]
    w_in = lax.all_gather(expert_in.reshape(slab, -1), "fsdp", axis=0, tiled=True)
    w_out = lax.all_gather(expert_out.reshape(slab, -1), "fsdp", axis=0, tiled=True)

    block_index = c ^ places
    positions = (
        block_index[:, None] * rows + jnp.arange(rows, dtype=jnp.int32)[None, :]
    ).reshape(length)
    inverse = ROPE_BASE ** (-jnp.arange(HEAD_DIM // 2, dtype=F32) / (HEAD_DIM // 2))
    angles = positions.astype(F32)[:, None] * inverse[None, :]
    cos = jnp.tile(jnp.cos(angles), (1, 2))
    sin = jnp.tile(jnp.sin(angles), (1, 2))
    qpos = positions[:, None]
    kpos = positions[None, :]

    n_one, queries, keys, values, heads_low, heads_high, lse = attend(
        shared_in, gain_one, w_qkv, cos, sin, qpos, kpos, width, q_wide
    )

    half_out = finish_o([after(part, heads_low) for part in came_o])
    other_out = swap_ctx(half_out, 1, ctx)
    w_output = jnp.concatenate(
        [
            jnp.where(first_half, half_out, other_out),
            jnp.where(first_half, other_out, half_out),
        ],
        axis=-1,
    )
    all_grad = gather_ctx(after(own_grad, heads_low), ctx)

    pieces = exchange_ctx(heads_low.reshape(ctx, rows, q_wide), ctx)
    attended = jnp.concatenate([pick(pieces, c ^ m) for m in range(ctx)], axis=-1)
    own_x = own.astype(F32)
    hidden = own_x + RESIDUAL * dot(attended, w_output)
    r_two = lax.rsqrt(jnp.mean(hidden * hidden, axis=-1, keepdims=True) + EPSILON)
    n_two = (hidden * r_two * gain_two).astype(BF)
    all_two = gather_ctx(n_two, ctx)
    all_attended = gather_ctx(after(attended, *all_two), ctx)

    def gates(values_low, mask):
        logits = dot(values_low, w_router)
        return jax.nn.softmax(jnp.where(mask > 0, logits, -1e30), axis=-1) * mask

    loc_named = columns(all_named, c * local, local).reshape(ctx, rows, local)
    before = (
        jnp.arange(rows, dtype=jnp.int32)[:, None] > jnp.arange(rows, dtype=jnp.int32)[None, :]
    ).astype(BF)
    rank = jnp.einsum(
        "tu,jue->jet", before, loc_named.astype(BF), preferred_element_type=F32
    )
    named_t = jnp.swapaxes(loc_named, 1, 2)
    slots = jnp.arange(MOST, dtype=F32)[:, None]
    hit = (rank[:, :, None, :] == slots) & (named_t[:, :, None, :] > 0)
    chooser = hit.astype(BF)
    chooser = chooser.reshape(ctx, local * MOST, rows)
    at_expert = jnp.stack([c * local, jnp.int32(experts)])
    x_slots, gy_slots, u, act, dy, g_slots, out_terms = expert_front(
        at_expert, all_named, chooser, w_router, w_in, all_two + all_grad
    )
    out_grad_w = lax.psum_scatter(out_terms, "fsdp", scatter_dimension=0, tiled=True)
    out_grad_w = out_grad_w.astype(F32).reshape(slab, local, FF)
    w_out = after(w_out, out_terms, *all_attended)
    back, moe, du = expert_back(
        at_expert, u, act, dy, gy_slots, g_slots, chooser, w_in, w_out
    )
    back_near = scatter_near(back, ctx)
    du = after(du, back_near)
    slots_all = ctx * MOST
    in_terms = jnp.concatenate(
        [
            dot(
                x_slots[e * slots_all : (e + 1) * slots_all],
                du[e * slots_all : (e + 1) * slots_all],
                ((0,), (0,)),
            ).astype(BF)
            for e in range(local)
        ],
        axis=-1,
    )
    in_grad = lax.psum_scatter(in_terms, "fsdp", scatter_dimension=0, tiled=True)
    in_grad = in_grad.astype(F32).reshape(slab, local, 2 * FF)
    back = scatter_far(*back_near, ctx)
    back = after(back, in_terms)
    moe_near = scatter_near(after(moe, back), ctx)

    dg = back[:, width : width + experts] + back[:, width + experts : width + 2 * experts]
    own_gates = gates(n_two, named)
    dlogits = (
        own_gates * (dg - jnp.sum(own_gates * dg, axis=-1, keepdims=True))
    ).astype(BF)
    dn_two = back[:, :width] + dot(dlogits, w_router, ((1,), (1,)))
    router_term = dot(n_two, dlogits, ((0,), (0,)))
    gain_two_term = jnp.sum(dn_two * hidden * r_two, axis=0)
    pulled = dn_two * gain_two
    dh = (
        own_grad.astype(F32)
        + r_two * pulled
        - hidden * r_two * r_two * r_two * jnp.mean(pulled * hidden, axis=-1, keepdims=True)
    )
    da, out_grad_w = lax.optimization_barrier(((RESIDUAL * dh).astype(BF), out_grad_w))
    do_own = dot(da, w_output, ((1,), (1,))).astype(BF)
    both = jnp.concatenate(
        [
            do_own.reshape(rows, ctx, q_wide),
            da.reshape(rows, ctx, width // ctx),
        ],
        axis=-1,
    )
    do_pieces = exchange_ctx(to_places(jnp.swapaxes(both, 0, 1)), ctx)
    do_heads = jnp.concatenate([do_pieces[k] for k in order], axis=0)
    moe_near = lax.optimization_barrier((moe_near, do_heads))[0]
    moe = scatter_far(*moe_near, ctx)

    extra = jnp.concatenate(
        [router_term, gain_two_term[:, None], jnp.zeros((width, 127 - experts), F32)], axis=-1
    )
    small, dn_one = attend_back(
        queries, keys, values, qpos, kpos, heads_high, lse, do_heads, cos, sin, n_one, w_qkv,
        gain_one.T, extra, all_attended,
    )
    dn_one, moe = lax.optimization_barrier((dn_one, moe))
    layer_out = (hidden + RESIDUAL * moe).astype(BF)
    dn_near = scatter_near(dn_one, ctx)
    came_s, finish_s = scatter_steps(small, fsdp, s)
    came_s = lax.optimization_barrier((dn_near, *came_s))[1:]
    small = finish_s(came_s).astype(BF)
    dn_one = scatter_far(*dn_near, ctx)
    small = lax.optimization_barrier((small, dn_one, in_grad))[0]
    small = gather_ctx(small, ctx)
    last = qkv_wide + width // ctx
    if kv_shared == 1 and q_wide == 128:
        query_out, key_out, value_out, output_out, rest = assemble(c[None], small)
    else:
        at = jnp.array([order.index(k) for k in range(ctx)], jnp.int32)
        small = jnp.stack(small, axis=0)
        shards = [pick(small, at[c ^ m]).astype(F32) for m in range(ctx)]
        output_out = jnp.concatenate([shard[:, qkv_wide:last] for shard in shards], axis=-1)
        query_out = jnp.concatenate([shard[:, :q_wide] for shard in shards], axis=-1)
        key_parts = [shard[:, q_wide : q_wide + HEAD_DIM] for shard in shards]
        value_parts = [shard[:, q_wide + HEAD_DIM : qkv_wide] for shard in shards]
        key_out = jnp.concatenate(
            [sum(key_parts[i : i + kv_shared]) for i in range(0, ctx, kv_shared)], axis=-1
        )
        value_out = jnp.concatenate(
            [sum(value_parts[i : i + kv_shared]) for i in range(0, ctx, kv_shared)], axis=-1
        )
        rest = jnp.sum(small[:, :, last:].astype(F32), axis=0)
    router_out = rest[:, :experts]
    gain_one_out = rest[:, 127]
    gain_two_out = rest[:, experts]

    pulled_one = dn_one * gain_one
    own_r = lax.rsqrt(jnp.mean(own_x * own_x, axis=-1, keepdims=True) + EPSILON)
    tokens_grad = (
        dh
        + own_r * pulled_one
        - own_x * own_r * own_r * own_r
        * jnp.mean(pulled_one * own_x, axis=-1, keepdims=True)
    )
    return (
        layer_out[None],
        tokens_grad[None],
        gain_one_out,
        query_out,
        key_out,
        value_out,
        output_out,
        gain_two_out,
        router_out,
        in_grad,
        out_grad_w,
    )


def solution(mesh):
    in_specs = (
        P("fsdp", "ctx", None),
        P("fsdp"),
        P("fsdp", None),
        P("fsdp", None),
        P("fsdp", None),
        P("fsdp", None),
        P("fsdp"),
        P("fsdp", None),
        P("fsdp", "ctx", None),
        P("fsdp", "ctx", None),
        P("fsdp", "ctx", None),
        P("fsdp", "ctx", None),
    )
    out_specs = (
        P("fsdp", "ctx", None),
        P("fsdp", "ctx", None),
        P("fsdp"),
        P("fsdp", None),
        P("fsdp", None),
        P("fsdp", None),
        P("fsdp", None),
        P("fsdp"),
        P("fsdp", None),
        P("fsdp", "ctx", None),
        P("fsdp", "ctx", None),
    )
    return jax.shard_map(
        per_device, mesh=mesh, in_specs=in_specs, out_specs=out_specs, check_vma=False
    )
```
